32 devices in a mesh: dp: 16 (over z, x, core), tensor: 2 (over y).
Axes of the slice: x: 2, y: 2, z: 4, core: 2. Of those that a mesh axis runs over, the one named last changes fastest.
Arguments:
- inputs: bfloat16 [4096, 2048], P('dp'), may hold values from -6 to 6
- cotangent: bfloat16 [4096, 2048], P('dp'), may hold values from -6 to 6
- segments: int32 [16, 256], P('dp'), may hold values from 0 to 3, never falling along the last dimension, each value on 1 to 128 neighbouring positions
- w_qkv: float32 [3, 8, 2048, 256], P(None, 'tensor', 'dp'), may hold values from -0.26516504 to 0.26516504
- w_out: float32 [8, 256, 2048], P('tensor', None, 'dp'), may hold values from -0.75 to 0.75
- w_up: float32 [2048, 8192], P('dp', 'tensor'), may hold values from -0.125 to 0.125
- w_down: float32 [8192, 2048], P('tensor', 'dp'), may hold values from -0.0625 to 0.0625
- b_qv: float32 [2, 8, 256], P(None, 'tensor', 'dp'), may hold values from -3 to 3
- b_up: float32 [8192], P(('tensor', 'dp')), may hold values from -3 to 3
- ln_gain: float32 [2, 2048], P(None, 'dp'), may hold values from 0.5 to 1.5
- ln_bias: float32 [2, 2048], P(None, 'dp'), may hold values from -3 to 3
- res_bias: float32 [2048], P('dp'), may hold values from -3 to 3
- m_qkv: float32 [3, 8, 2048, 256], P(None, 'tensor', 'dp'), may hold values from -3 to 3
- m_out: float32 [8, 256, 2048], P('tensor', None, 'dp'), may hold values from -3 to 3
- m_up: float32 [2048, 8192], P('dp', 'tensor'), may hold values from -3 to 3
- m_down: float32 [8192, 2048], P('tensor', 'dp'), may hold values from -3 to 3
- m_bqv: float32 [2, 8, 256], P(None, 'tensor', 'dp'), may hold values from -3 to 3
- m_bup: float32 [8192], P(('tensor', 'dp')), may hold values from -3 to 3
- m_gain: float32 [2, 2048], P(None, 'dp'), may hold values from -3 to 3
- m_lnbias: float32 [2, 2048], P(None, 'dp'), may hold values from -3 to 3
- m_res: float32 [2048], P('dp'), may hold values from -3 to 3
Outputs:
- output: bfloat16 [4096, 2048], P('dp')
- input_grad: float32 [4096, 2048], P('dp')
- grad_qkv: float32 [3, 8, 2048, 256], P(None, 'tensor', 'dp')
- grad_out: float32 [8, 256, 2048], P('tensor', None, 'dp')
- grad_up: float32 [2048, 8192], P('dp', 'tensor')
- grad_down: float32 [8192, 2048], P('tensor', 'dp')
- grad_bqv: float32 [2, 8, 256], P(None, 'tensor', 'dp')
- grad_bup: float32 [8192], P(('tensor', 'dp'))
- grad_gain: float32 [2, 2048], P(None, 'dp')
- grad_lnbias: float32 [2, 2048], P(None, 'dp')
- grad_res: float32 [2048], P('dp')
- new_qkv: float32 [3, 8, 2048, 256], P(None, 'tensor', 'dp')
- new_out: float32 [8, 256, 2048], P('tensor', None, 'dp')
- new_up: float32 [2048, 8192], P('dp', 'tensor')
- new_down: float32 [8192, 2048], P('tensor', 'dp')
- new_bqv: float32 [2, 8, 256], P(None, 'tensor', 'dp')
- new_bup: float32 [8192], P(('tensor', 'dp'))
- new_gain: float32 [2, 2048], P(None, 'dp')
- new_lnbias: float32 [2, 2048], P(None, 'dp')
- new_res: float32 [2048], P('dp')
- mom_qkv: float32 [3, 8, 2048, 256], P(None, 'tensor', 'dp')
- mom_out: float32 [8, 256, 2048], P('tensor', None, 'dp')
- mom_up: float32 [2048, 8192], P('dp', 'tensor')
- mom_down: float32 [8192, 2048], P('tensor', 'dp')
- mom_bqv: float32 [2, 8, 256], P(None, 'tensor', 'dp')
- mom_bup: float32 [8192], P(('tensor', 'dp'))
- mom_gain: float32 [2, 2048], P(None, 'dp')
- mom_lnbias: float32 [2, 2048], P(None, 'dp')
- mom_res: float32 [2048], P('dp')
The draws below stay inside these ranges and needn't reach their ends.
Inputs may be any that keep to these rules, and one draw needn't show every extreme that they name: `segments`: segment numbers never fall along a row; a segment holds 1 to 128 tokens, and some segment holds exactly 128.
All inputs are finite; a program needn't handle non-finite values.
Results may differ from the reference program's by a relative error of at most 0.014.
Values may be sent and summed in bfloat16 or wider, within the bound.
No kernel may reach another device: no remote copies, remote signals or barrier semaphores. Data moves between devices by JAX's collectives and lax.ppermute only.
A program may use at most 384 MiB of HBM per device.

```python
import math
import jax
import jax.numpy as jnp
import numpy as np
from jax import lax

MODEL_WIDTH = 2048
HD = 256
H = 8
FF = 8192
ROT = 64
DOCS = 4
NS_ITERS = 5
LEN = 256
SEQS = 16
TOKENS = 4096
N_TENSOR = 2


def draw_w_qkv(key, part):
    weights_base = jax.random.truncated_normal(key, -4.0, 4.0, (3, H, MODEL_WIDTH, HD), jnp.float32) * float(MODEL_WIDTH) ** (-0.5)
    return weights_base


def raised(result, own_key, source, target, blocks, factor):
    def block_of(axis_at):
        return (jnp.arange(result.shape[axis_at]) // (result.shape[axis_at] // blocks)).reshape((-1,) + (1,) * (result.ndim - 1 - axis_at))

    first = jax.random.permutation(own_key, blocks)[block_of(target)]
    second = (block_of(target) + blocks // 2) % blocks
    return jnp.where((block_of(source) == first) | (block_of(source) == second), factor * result, result)


def steps_of(own_key, dims, cuts, low, largest):
    gain, own = 1.0, jax.random.fold_in(own_key, 6)
    for dim, blocks in cuts:
        heights = jnp.exp(jax.random.uniform(jax.random.fold_in(own, dim), (blocks,), jnp.float32, low / len(cuts), largest / len(cuts)))
        gain = gain * jnp.repeat(heights, dims[dim] // blocks).reshape([-1 if axis == dim else 1 for axis in range(len(dims))])
    return gain


def length_profile(amount, total, bound, skew):
    portions = [(1 << 20) // math.isqrt(standing ** skew) + 1 for standing in range(2, amount + 1)]
    spare, given = total - bound - (amount - 1), [1] * (amount - 1)
    while spare > 0:
        candidates = [i for i in range(amount - 1) if given[i] < bound]
        whole, left = sum([portions[i] for i in candidates]), spare
        for i in candidates:
            extra = min(bound - given[i], max(1, left * portions[i] // whole), spare)
            given[i] = given[i] + extra
            spare = spare - extra
    return np.array([bound] + given)


def uneven(stream_key, count, total, bound, slope):
    if count == 2:
        one = jax.random.randint(stream_key, (), max(1, total - bound), min(bound, total - 1) + 1)
        return jnp.stack([one, total - one])
    lengths = jnp.asarray(length_profile(count, total, bound, slope), jnp.int32)
    couples = (count - 1) // 2
    source_of, sink = lengths[1:1 + 2 * couples:2], lengths[2:2 + 2 * couples:2]
    margin = jnp.minimum(source_of - 1, bound - sink)
    shifted = jax.random.randint(jax.random.fold_in(stream_key, 1), (couples,), 0, 1 << 20) % (margin + 1)
    lengths = lengths.at[1:1 + 2 * couples:2].set(source_of - shifted).at[2:2 + 2 * couples:2].set(sink + shifted)
    return lengths[jax.random.permutation(jax.random.fold_in(stream_key, 2), count)]


def gaussian(stream_key, extent, deviation, bound, split=(), held_as=jnp.bfloat16):
    array = deviation * jax.random.normal(stream_key, extent, jnp.float32)
    if split:
        array = array * steps_of(stream_key, extent, split, -0.22, 0.18)
    return jnp.clip(array, -bound, bound).astype(held_as)


def bell_draw_with(stream_key, shape, scale, limit, shards, heavy, kind=jnp.bfloat16):
    array = scale * jax.random.normal(stream_key, shape, jnp.float32)
    if shards:
        array = array * steps_of(stream_key, shape, shards, -0.22, 0.18)
    return jnp.clip(raised(array, jax.random.fold_in(stream_key, 3), *heavy), -limit, limit).astype(kind)


def setup_inputs(seed: int = 0) -> dict:
    splits = jax.random.split(jax.random.key(seed), 22)
    inputs = bell_draw_with(splits[0], (TOKENS, MODEL_WIDTH), 1.0, 6.0, ((0, 16),), (0, 1, 16, 2.0))
    cotangent = bell_draw_with(splits[1], (TOKENS, MODEL_WIDTH), 1.0, 6.0, ((0, 16),), (0, 1, 16, 2.0))
    segments = jax.vmap(lambda own: jnp.searchsorted(jnp.cumsum(uneven(own, DOCS, LEN, LEN // 2, 2)), jnp.arange(LEN), side="right"))(jax.random.split(splits[2], SEQS)).reshape((SEQS, LEN)).astype(jnp.int32)
    w_qkv = draw_w_qkv(jax.random.fold_in(splits[21], 71), 0)
    w_out = gaussian(splits[4], (H, HD, MODEL_WIDTH), 64 ** -0.5, 0.75, ((0, 2), (2, 16)), jnp.float32)
    w_up = gaussian(splits[5], (MODEL_WIDTH, FF), MODEL_WIDTH ** -0.5, 0.125, ((0, 16), (1, 2)), jnp.float32)
    w_down = gaussian(splits[6], (FF, MODEL_WIDTH), FF ** -0.5, 0.0625, ((0, 2), (1, 16)), jnp.float32)
    b_qv = gaussian(splits[7], (2, H, HD), 0.5, 3.0, ((1, 2), (2, 16)), jnp.float32)
    b_up = gaussian(splits[8], (FF,), 0.5, 3.0, ((0, 32),), jnp.float32)
    ln_gain = jnp.clip(1.0 + 0.1 * jax.random.normal(splits[9], (2, MODEL_WIDTH), jnp.float32), 0.5, 1.5)
    ln_bias = gaussian(splits[10], (2, MODEL_WIDTH), 0.5, 3.0, ((1, 16),), jnp.float32)
    res_bias = gaussian(splits[11], (MODEL_WIDTH,), 0.5, 3.0, ((0, 16),), jnp.float32)
    m_qkv = gaussian(splits[12], (3, H, MODEL_WIDTH, HD), 0.5, 3.0, ((1, 2), (2, 16)), jnp.float32)
    m_out = gaussian(splits[13], (H, HD, MODEL_WIDTH), 0.5, 3.0, ((0, 2), (2, 16)), jnp.float32)
    m_up = gaussian(splits[14], (MODEL_WIDTH, FF), 0.5, 3.0, ((0, 16), (1, 2)), jnp.float32)
    m_down = gaussian(splits[15], (FF, MODEL_WIDTH), 0.5, 3.0, ((0, 2), (1, 16)), jnp.float32)
    m_bqv = gaussian(splits[16], (2, H, HD), 0.5, 3.0, ((1, 2), (2, 16)), jnp.float32)
    m_bup = gaussian(splits[17], (FF,), 0.5, 3.0, ((0, 32),), jnp.float32)
    m_gain = gaussian(splits[18], (2, MODEL_WIDTH), 0.5, 3.0, ((1, 16),), jnp.float32)
    m_lnbias = gaussian(splits[19], (2, MODEL_WIDTH), 0.5, 3.0, ((1, 16),), jnp.float32)
    m_res = gaussian(splits[20], (MODEL_WIDTH,), 0.5, 3.0, ((0, 16),), jnp.float32)
    return dict(inputs=inputs, cotangent=cotangent, segments=segments, w_qkv=w_qkv, w_out=w_out, w_up=w_up, w_down=w_down, b_qv=b_qv, b_up=b_up, ln_gain=ln_gain, ln_bias=ln_bias, res_bias=res_bias, m_qkv=m_qkv, m_out=m_out, m_up=m_up, m_down=m_down, m_bqv=m_bqv, m_bup=m_bup, m_gain=m_gain, m_lnbias=m_lnbias, m_res=m_res)


norm_eps = 1e-05
momentum_beta = 0.9
matrix_rate = 0.1
vector_rate = 0.4
coef_one = 3.4445
coef_two = -4.775
coef_three = 2.0315
big_negative = -1e+30

def to_single_float(array_in):
    return array_in.astype(jnp.float32)

def layer_normalize(values, gain_row, bias_row):
    centred = values - lax.optimization_barrier(jnp.mean(values, axis=-1, keepdims=True))
    inv_std = lax.rsqrt(lax.optimization_barrier(jnp.mean(centred * centred, axis=-1, keepdims=True)) + norm_eps)
    x_hat = centred * inv_std
    return ((x_hat * gain_row + bias_row).astype(jnp.bfloat16), x_hat, inv_std)

def norm_reverse_pass(grad_in, x_hat, inv_std, gain_row):
    scaled_g = grad_in * gain_row
    mean_g = lax.optimization_barrier(jnp.mean(scaled_g, axis=-1, keepdims=True))
    mean_gx = lax.optimization_barrier(jnp.mean(scaled_g * x_hat, axis=-1, keepdims=True))
    return (inv_std * (scaled_g - mean_g - x_hat * mean_gx), lax.optimization_barrier(jnp.sum(grad_in * x_hat, axis=0)), lax.optimization_barrier(jnp.sum(grad_in, axis=0)))

def rotary_tables(seg_ids, rot_dims):
    order_idx = jnp.arange(seg_ids.shape[0], dtype=jnp.int32)
    allowed = (seg_ids[:, None] == seg_ids[None, :]) & (order_idx[:, None] >= order_idx[None, :])
    position = (lax.optimization_barrier(jnp.sum(allowed.astype(jnp.int32), axis=1)) - 1).astype(jnp.float32)
    freq_idx = jnp.arange(rot_dims // 2, dtype=jnp.float32)
    inv_freq = jnp.exp(freq_idx * (-2.0 * math.log(10000.0) / rot_dims))
    angles = position[:, None] * inv_freq[None, :]
    return (allowed, jnp.cos(angles), jnp.sin(angles))

def rotate(values, cos_tab, sin_tab):
    half_dim = cos_tab.shape[1]
    low_part = values[..., :half_dim]
    high_part = values[..., half_dim:2 * half_dim]
    cos_b = cos_tab[:, None, :]
    sin_b = sin_tab[:, None, :]
    return jnp.concatenate([low_part * cos_b - high_part * sin_b, high_part * cos_b + low_part * sin_b, values[..., 2 * half_dim:]], axis=-1)

def unrotate(values, cos_tab, sin_tab):
    half_dim = cos_tab.shape[1]
    low_part = values[..., :half_dim]
    high_part = values[..., half_dim:2 * half_dim]
    cos_b = cos_tab[:, None, :]
    sin_b = sin_tab[:, None, :]
    return jnp.concatenate([low_part * cos_b + high_part * sin_b, high_part * cos_b - low_part * sin_b, values[..., 2 * half_dim:]], axis=-1)

def gelu_grad(pre_act):
    cdf_val = 0.5 * (1.0 + lax.erf(pre_act * (1.0 / math.sqrt(2.0))))
    pdf_val = jnp.exp(-0.5 * pre_act * pre_act) * (1.0 / math.sqrt(2.0 * math.pi))
    return cdf_val + pre_act * pdf_val

def masked_scores(q_rot, k_rot, allowed, scaling):
    scores = jnp.einsum('lhe,mhe->hlm', to_single_float(q_rot), to_single_float(k_rot)) * scaling
    return jnp.where(allowed[None, :, :], scores, big_negative)

def branch_halves_total(parts):
    return lax.optimization_barrier(jnp.sum(to_single_float(lax.optimization_barrier(parts.astype(jnp.bfloat16))), axis=0))

def sequence_pass(x_seq, cot_seq, seg_ids, params):
    wqkv, wout, up_weight, wdown, bqv_f, bup_f, gain_single, norm_bias_single, rbias_f = params
    length_value = x_seq.shape[0]
    heads_half = H // N_TENSOR
    hidden_portion = FF // N_TENSOR
    scaling = float(HD) ** (-0.5)
    allowed, cos_tab, sin_tab = rotary_tables(seg_ids, ROT)
    input_single = to_single_float(x_seq)
    first_activation, first_normalized, first_inverse_deviation = layer_normalize(input_single, gain_single[0], norm_bias_single[0])
    second_activation, second_normalized, second_inverse_deviation = layer_normalize(input_single, gain_single[1], norm_bias_single[1])
    qkv_f = jnp.einsum('ld,chde->clhe', to_single_float(first_activation), to_single_float(wqkv))
    q_rot = rotate(qkv_f[0] + bqv_f[0], cos_tab, sin_tab).astype(jnp.bfloat16)
    k_rot = rotate(qkv_f[1], cos_tab, sin_tab).astype(jnp.bfloat16)
    v_bf = (qkv_f[2] + bqv_f[1]).astype(jnp.bfloat16)
    masked = masked_scores(q_rot, k_rot, allowed, scaling)
    row_top = lax.optimization_barrier(jnp.max(masked, axis=-1, keepdims=True))
    log_sum = row_top + jnp.log(lax.optimization_barrier(jnp.sum(jnp.exp(masked - row_top), axis=-1, keepdims=True)))
    p_bf = jnp.exp(masked - log_sum).astype(jnp.bfloat16)
    o_bf = jnp.einsum('hlm,mhe->lhe', to_single_float(p_bf), to_single_float(v_bf)).astype(jnp.bfloat16)
    pre_act = jnp.dot(second_activation, up_weight, preferred_element_type=jnp.float32) + bup_f
    h_bf = jax.nn.gelu(pre_act, approximate=False).astype(jnp.bfloat16)
    attn_halves = jnp.einsum('lrhe,rhed->rld', to_single_float(o_bf.reshape(length_value, N_TENSOR, heads_half, HD)), to_single_float(wout.reshape(N_TENSOR, heads_half, HD, MODEL_WIDTH)))
    mlp_halves = jnp.einsum('lrf,rfd->rld', to_single_float(h_bf.reshape(length_value, N_TENSOR, hidden_portion)), to_single_float(wdown.reshape(N_TENSOR, hidden_portion, MODEL_WIDTH)))
    branch = branch_halves_total(attn_halves + mlp_halves)
    output_seq = (input_single + branch + rbias_f).astype(jnp.bfloat16)
    dy_f = to_single_float(cot_seq)
    grad_res = lax.optimization_barrier(jnp.sum(dy_f, axis=0))
    grad_down = jnp.dot(h_bf.T, cot_seq, preferred_element_type=jnp.float32)
    dh_f = jnp.dot(cot_seq, wdown.T, preferred_element_type=jnp.float32)
    du_f = dh_f * gelu_grad(pre_act)
    grad_bup = lax.optimization_barrier(jnp.sum(du_f, axis=0))
    upward_grad_brain = du_f.astype(jnp.bfloat16)
    grad_up = jnp.dot(second_activation.T, upward_grad_brain, preferred_element_type=jnp.float32)
    grad_out = jnp.einsum('lhe,ld->hed', to_single_float(o_bf), dy_f)
    do_bf = jnp.einsum('ld,hed->lhe', dy_f, to_single_float(wout)).astype(jnp.bfloat16)
    masked_again = masked_scores(q_rot, k_rot, allowed, scaling)
    prob_f = jnp.exp(masked_again - log_sum)
    prob_bf = prob_f.astype(jnp.bfloat16)
    dprob_f = jnp.einsum('lhe,mhe->hlm', to_single_float(do_bf), to_single_float(v_bf))
    delta_rows = lax.optimization_barrier(jnp.sum(to_single_float(do_bf) * to_single_float(o_bf), axis=-1))
    dscore_bf = (prob_f * (dprob_f - jnp.transpose(delta_rows)[:, :, None]) * scaling).astype(jnp.bfloat16)
    dq_f = unrotate(jnp.einsum('hlm,mhe->lhe', to_single_float(dscore_bf), to_single_float(k_rot)), cos_tab, sin_tab)
    dk_f = unrotate(jnp.einsum('hlm,lhe->mhe', to_single_float(dscore_bf), to_single_float(q_rot)), cos_tab, sin_tab)
    dv_f = jnp.einsum('hlm,lhe->mhe', to_single_float(prob_bf), to_single_float(do_bf))
    grad_bqv = jnp.stack([lax.optimization_barrier(jnp.sum(dq_f, axis=0)), lax.optimization_barrier(jnp.sum(dv_f, axis=0))])
    dqkv_bf = jnp.stack([dq_f, dk_f, dv_f]).astype(jnp.bfloat16)
    grad_qkv = jnp.einsum('ld,clhe->chde', to_single_float(first_activation), to_single_float(dqkv_bf))
    first_activation_grad = branch_halves_total(jnp.einsum('clrhe,crhde->rld', to_single_float(dqkv_bf.reshape(3, length_value, N_TENSOR, heads_half, HD)), to_single_float(wqkv.reshape(3, N_TENSOR, heads_half, MODEL_WIDTH, HD))))
    second_activation_grad = branch_halves_total(jnp.einsum('iqs,nqs->qin', to_single_float(upward_grad_brain.reshape(length_value, N_TENSOR, hidden_portion)), to_single_float(up_weight.reshape(MODEL_WIDTH, N_TENSOR, hidden_portion))))
    first_input_grad, first_gain, first_bias = norm_reverse_pass(first_activation_grad, first_normalized, first_inverse_deviation, gain_single[0])
    second_input_grad, second_gain, second_bias = norm_reverse_pass(second_activation_grad, second_normalized, second_inverse_deviation, gain_single[1])
    input_seq = dy_f + first_input_grad + second_input_grad
    grads = (grad_qkv, grad_out, grad_up, grad_down, grad_bqv, grad_bup, jnp.stack([first_gain, second_gain]), jnp.stack([first_bias, second_bias]), grad_res)
    return (output_seq, input_seq, grads)

def to_blocks(like_qkv, like_out, like_up, like_down):
    head_dim = like_qkv.shape[3]
    part_qkv = like_qkv.reshape(-1, like_qkv.shape[2], head_dim)
    part_up = jnp.transpose(like_up.reshape(like_up.shape[0], -1, head_dim), (1, 0, 2))
    part_out = jnp.transpose(like_out, (0, 2, 1))
    part_down = jnp.transpose(like_down.reshape(-1, head_dim, like_down.shape[1]), (0, 2, 1))
    return jnp.concatenate([part_qkv, part_up, part_out, part_down], axis=0)

def from_blocks(blocks, like_qkv, like_out, like_up, like_down):
    head_dim = like_qkv.shape[3]
    count_qkv = like_qkv.shape[0] * like_qkv.shape[1]
    count_up = like_up.shape[1] // head_dim
    count_out = like_out.shape[0]
    start_out = count_qkv + count_up
    start_down = start_out + count_out
    part_qkv = blocks[:count_qkv].reshape(like_qkv.shape)
    part_up = jnp.transpose(blocks[count_qkv:start_out], (1, 0, 2)).reshape(like_up.shape)
    part_out = jnp.transpose(blocks[start_out:start_down], (0, 2, 1))
    part_down = jnp.transpose(blocks[start_down:], (0, 2, 1)).reshape(like_down.shape)
    return (part_qkv, part_out, part_up, part_down)

def orthogonal(blocks):
    norm_val = jnp.sqrt(lax.optimization_barrier(jnp.sum(blocks * blocks, axis=(1, 2), keepdims=True))) + 1e-07
    current = blocks / norm_val
    for turn_idx in range(NS_ITERS):
        gram_now = jnp.einsum('nde,ndf->nef', current, current, precision=lax.Precision.HIGHEST)
        poly_mat = coef_two * gram_now + coef_three * jnp.einsum('nef,nfg->neg', gram_now, gram_now, precision=lax.Precision.HIGHEST)
        current = coef_one * current + jnp.einsum('nde,nef->ndf', current, poly_mat, precision=lax.Precision.HIGHEST)
    return current

def reference(inputs, cotangent, segments, w_qkv, w_out, w_up, w_down, b_qv, b_up, ln_gain, ln_bias, res_bias, m_qkv, m_out, m_up, m_down, m_bqv, m_bup, m_gain, m_lnbias, m_res):
    matrices = tuple((item.astype(jnp.bfloat16) for item in (w_qkv, w_out, w_up, w_down)))
    vectors = tuple((to_single_float(lax.optimization_barrier(item.astype(jnp.bfloat16))) for item in (b_qv, b_up, ln_gain, ln_bias, res_bias)))
    params = matrices + vectors
    seq_count = segments.shape[0]
    x_seqs = inputs.reshape(seq_count, LEN, MODEL_WIDTH)
    cot_seqs = cotangent.reshape(seq_count, LEN, MODEL_WIDTH)
    zero_sums = tuple((jnp.zeros(item.shape, jnp.float32) for item in (w_qkv, w_out, w_up, w_down, b_qv, b_up, ln_gain, ln_bias, res_bias)))

    def step_fn(carried, pieces):
        out_seq, in_seq, grads = sequence_pass(pieces[0], pieces[1], pieces[2], params)
        return (tuple((acc_item + new_item for acc_item, new_item in zip(carried, grads))), (out_seq, in_seq))
    total_grads, (out_all, in_all) = lax.scan(step_fn, zero_sums, (x_seqs, cot_seqs, segments))
    grad_scale = float(TOKENS) ** (-0.5)
    grads = tuple((item * grad_scale for item in total_grads))
    olds = (m_qkv, m_out, m_up, m_down, m_bqv, m_bup, m_gain, m_lnbias, m_res)
    moms = tuple((momentum_beta * mom_item + grad_item for mom_item, grad_item in zip(olds, grads)))
    new_vectors = tuple((param_old - vector_rate * mom_item for param_old, mom_item in zip((b_qv, b_up, ln_gain, ln_bias, res_bias), moms[4:])))
    ortho = orthogonal(to_blocks(moms[0], moms[1], moms[2], moms[3]))
    updates = from_blocks(ortho, moms[0], moms[1], moms[2], moms[3])
    step_size = matrix_rate * 0.2 * math.sqrt(MODEL_WIDTH)
    new_mats = tuple((param_old - step_size * upd_item for param_old, upd_item in zip((w_qkv, w_out, w_up, w_down), updates)))
    return (out_all.reshape(TOKENS, MODEL_WIDTH), in_all.reshape(TOKENS, MODEL_WIDTH), grads[0], grads[1], grads[2], grads[3], grads[4], grads[5], grads[6], grads[7], grads[8], new_mats[0], new_mats[1], new_mats[2], new_mats[3], new_vectors[0], new_vectors[1], new_vectors[2], new_vectors[3], new_vectors[4], moms[0], moms[1], moms[2], moms[3], moms[4], moms[5], moms[6], moms[7], moms[8])
```

```python
import math

import jax
import jax.numpy as jnp
from jax import lax
from jax.experimental import pallas as pl
from jax.experimental.pallas import tpu as pltpu
from jax.sharding import PartitionSpec as P

MODEL_WIDTH = 2048
ROT = 64
NS_ITERS = 5

norm_eps = 1e-05
momentum_beta = 0.9
matrix_rate = 0.1
vector_rate = 0.4
coef_one = 3.4445
coef_two = -4.775
coef_three = 2.0315
big_negative = -1e30

bf16 = jnp.bfloat16
f32 = jnp.float32

INTERPRET = False


def dot(a, b, dims):
    return lax.dot_general(a, b, (dims, ((), ())), preferred_element_type=f32)


def nn(a, b):
    return dot(a, b, ((1,), (0,)))


def nt(a, b):
    return dot(a, b, ((1,), (1,)))


def tn(a, b):
    return dot(a, b, ((0,), (0,)))


def after(value, token):
    return lax.optimization_barrier((value, token))[0]


def snake(chips):
    return list(range(0, chips, 2)) + list(range(chips - 1, 0, -2))


class Ring:
    def __init__(self, dp):
        self.chips = dp // 2
        order = snake(self.chips)
        self.order = jnp.array(order, jnp.int32)
        place = [order.index(i) for i in range(self.chips)]
        index = lax.axis_index("dp")
        self.core = index % 2
        self.chip = index // 2
        self.me = jnp.array(place, jnp.int32)[self.chip]
        links = [(order[i], order[(i + 1) % self.chips]) for i in range(self.chips)]
        self.up = [(2 * a + c, 2 * b + c) for a, b in links for c in range(2)]
        self.down = [(b, a) for a, b in self.up]
        self.pair = [(i, i ^ 1) for i in range(dp)]

    def at(self, offset):
        return self.order[(self.me + offset + 2 * self.chips) % self.chips]

    def swap(self, value):
        return lax.ppermute(value, "dp", self.pair)

    def by_core(self, mine, other):
        first = self.core == 0
        return jnp.where(first, mine, other), jnp.where(first, other, mine)

    def gather(self, shard, pieces, token=None):
        rows, cols = shard.shape
        half = cols // 2
        mine = lax.dynamic_slice(shard, (0, self.core * half), (rows, half))
        theirs = lax.dynamic_slice(shard, (0, (1 - self.core) * half), (rows, half))
        low, high = self.by_core(mine, self.swap(theirs))
        if token is not None:
            low, high = after(low, token), after(high, token)
        width = half // pieces
        out = jnp.zeros((2 * self.chips * rows, half), shard.dtype)
        start = self.chip * 2 * rows
        out = lax.dynamic_update_slice(out, low, (start, 0))
        out = lax.dynamic_update_slice(out, high, (start + rows, 0))
        lows = [low[:, i * width : (i + 1) * width] for i in range(pieces)]
        highs = [high[:, i * width : (i + 1) * width] for i in range(pieces)]
        marks = []
        for step in range(1, self.chips):
            from_low = self.at(-step) * 2 * rows
            from_high = self.at(step) * 2 * rows + rows
            for i in range(pieces):
                lows[i] = lax.ppermute(lows[i], "dp", self.up)
                highs[i] = lax.ppermute(highs[i], "dp", self.down)
                out = lax.dynamic_update_slice(out, lows[i], (from_low, i * width))
                out = lax.dynamic_update_slice(out, highs[i], (from_high, i * width))
            marks.append(lows[-1])
        return out, marks

    def reduce(self, grad, rows, pieces):
        half = grad.shape[1]
        width = half // pieces

        def chunk(offset, high, i):
            start = self.at(offset) * 2 * rows + high * rows
            return lax.dynamic_slice(grad, (start, i * width), (rows, width))

        lows = [chunk(-1, 0, i) for i in range(pieces)]
        highs = [chunk(1, 1, i) for i in range(pieces)]
        for step in range(1, self.chips):
            last = step == self.chips - 1
            for i in range(pieces):
                low = lax.ppermute(lows[i], "dp", self.up)
                high = lax.ppermute(highs[i], "dp", self.down)
                low = low.astype(f32) + chunk(-1 - step, 0, i).astype(f32)
                high = high.astype(f32) + chunk(1 + step, 1, i).astype(f32)
                lows[i] = low if last else low.astype(bf16)
                highs[i] = high if last else high.astype(bf16)
        low = jnp.concatenate(lows, axis=1)
        high = jnp.concatenate(highs, axis=1)
        mine, theirs = self.by_core(low, high)
        left, right = self.by_core(mine, self.swap(theirs))
        return jnp.concatenate([left, right], axis=1)


def over_tensor(value):
    if lax.axis_size("tensor") == 2:
        return value.astype(f32) + lax.ppermute(value, "tensor", [(0, 1), (1, 0)]).astype(f32)
    return lax.psum(value, "tensor").astype(f32)


def combine(ring, partial):
    tokens = partial.shape[0] // 2
    theirs = ring.swap(partial[tokens:].astype(bf16))
    return over_tensor((partial[:tokens] + theirs.astype(f32)).astype(bf16))


def normalize(values):
    centred = values - jnp.mean(values, axis=-1, keepdims=True)
    inv_std = lax.rsqrt(jnp.mean(centred * centred, axis=-1, keepdims=True) + norm_eps)
    return centred * inv_std, inv_std


def norm_reverse_pass(grad_in, x_hat, inv_std, gain_row):
    scaled_g = grad_in * gain_row
    mean_g = jnp.mean(scaled_g, axis=-1, keepdims=True)
    mean_gx = jnp.mean(scaled_g * x_hat, axis=-1, keepdims=True)
    return (
        inv_std * (scaled_g - mean_g - x_hat * mean_gx),
        jnp.sum(grad_in * x_hat, axis=0),
        jnp.sum(grad_in, axis=0),
    )


def rotary_tables(seg_ids, rot_dims):
    order_idx = jnp.arange(seg_ids.shape[1], dtype=jnp.int32)
    causal = order_idx[:, None] >= order_idx[None, :]
    allowed = (seg_ids[:, :, None] == seg_ids[:, None, :]) & causal[None]
    position = (jnp.sum(allowed.astype(jnp.int32), axis=2) - 1).astype(f32)
    freq_idx = jnp.arange(rot_dims // 2, dtype=f32)
    inv_freq = jnp.exp(freq_idx * (-2.0 * math.log(10000.0) / rot_dims))
    angles = position[:, :, None] * inv_freq
    return allowed, jnp.cos(angles)[:, :, None, :], jnp.sin(angles)[:, :, None, :]


def rotate(values, cos_b, sin_b):
    half_dim = cos_b.shape[-1]
    low = values[..., :half_dim]
    high = values[..., half_dim : 2 * half_dim]
    return jnp.concatenate(
        [low * cos_b - high * sin_b, high * cos_b + low * sin_b, values[..., 2 * half_dim :]], axis=-1
    )


def gelu_parts(pre_act):
    cdf = 0.5 * (1.0 + lax.erf(pre_act * (1.0 / math.sqrt(2.0))))
    pdf = jnp.exp(-0.5 * pre_act * pre_act) * (1.0 / math.sqrt(2.0 * math.pi))
    return pre_act * cdf, cdf + pre_act * pdf


def attention(q, k, v, allowed, scaling):
    scores = jnp.einsum("slhe,smhe->shlm", q, k, preferred_element_type=f32) * scaling
    masked = jnp.where(allowed[:, None], scores, big_negative)
    top = jnp.max(masked, axis=-1, keepdims=True)
    log_sum = top + jnp.log(jnp.sum(jnp.exp(masked - top), axis=-1, keepdims=True))
    prob = jnp.exp(masked - log_sum)
    out = jnp.einsum("shlm,smhe->slhe", prob.astype(bf16), v, preferred_element_type=f32)
    return out.astype(bf16), prob


def attention_back(q, k, v, o, do, prob, scaling):
    dprob = jnp.einsum("slhe,smhe->shlm", do, v, preferred_element_type=f32)
    delta = jnp.sum(do.astype(f32) * o.astype(f32), axis=-1)
    dscore = (prob * (dprob - jnp.transpose(delta, (0, 2, 1))[..., None]) * scaling).astype(bf16)
    dq = jnp.einsum("shlm,smhe->slhe", dscore, k, preferred_element_type=f32)
    dk = jnp.einsum("shlm,slhe->smhe", dscore, q, preferred_element_type=f32)
    dv = jnp.einsum("shlm,slhe->smhe", prob.astype(bf16), do, preferred_element_type=f32)
    return dq, dk, dv


def series_kernel(gram_ref, out_ref):
    def mul(a, b):
        return jnp.dot(a, b, preferred_element_type=f32, precision=lax.Precision.HIGHEST)

    gram = gram_ref[0]
    size = gram.shape[0]
    row = lax.broadcasted_iota(jnp.int32, (size, size), 0)
    col = lax.broadcasted_iota(jnp.int32, (size, size), 1)
    diagonal = row == col
    trace = jnp.sum(jnp.where(diagonal, gram, 0.0), axis=(0, 1), keepdims=True)
    inverse = 1.0 / (jnp.sqrt(trace) + 1e-07)
    gram = gram * inverse * inverse
    total = jnp.where(diagonal, 1.0, 0.0) * inverse
    for turn in range(NS_ITERS):
        poly = coef_two * gram + coef_three * mul(gram, gram)
        if turn == 0:
            total = coef_one * total + poly * inverse
        else:
            total = coef_one * total + mul(total, poly)
        if turn < NS_ITERS - 1:
            once = coef_one * gram + mul(gram, poly)
            gram = coef_one * once + mul(once, poly)
    out_ref[0] = total.astype(out_ref.dtype)


def series(grams):
    count, size, _ = grams.shape
    spec = pl.BlockSpec((1, size, size), lambda i: (i, 0, 0))
    return pl.pallas_call(
        series_kernel,
        grid=(count,),
        in_specs=[spec],
        out_specs=spec,
        out_shape=jax.ShapeDtypeStruct(grams.shape, bf16),
        interpret=INTERPRET,
        name="series",
    )(grams)


def muon_update(momentum, head_dim):
    rows, cols = momentum.shape
    count = cols // head_dim
    dp = lax.axis_size("dp")
    slots = -(-count // dp)
    blocks = jnp.transpose(momentum.astype(bf16).reshape(rows, count, head_dim), (1, 0, 2))
    if slots * dp != count:
        blocks = jnp.pad(blocks, ((0, slots * dp - count), (0, 0), (0, 0)))
    blocks = blocks.reshape(dp, slots, rows, head_dim)
    whole = lax.all_to_all(blocks, "dp", split_axis=0, concat_axis=2, tiled=True)[0]
    grams = jnp.einsum("ndf,ndg->nfg", whole, whole, preferred_element_type=f32)
    done = jnp.einsum("ndf,nfg->ndg", whole, series(grams), preferred_element_type=f32).astype(bf16)
    back = lax.all_to_all(done[None], "dp", split_axis=2, concat_axis=0, tiled=True)
    back = back.reshape(slots * dp, rows, head_dim)[:count]
    return jnp.transpose(back, (1, 0, 2)).reshape(rows, cols)


def pack_attention(qkv, out):
    kinds, heads, rows, size = qkv.shape
    both = jnp.concatenate([qkv, jnp.transpose(out, (0, 2, 1))[None]], axis=0)
    both = both.reshape(kinds + 1, 2, heads // 2, rows, size)
    return jnp.transpose(both, (3, 1, 0, 2, 4)).reshape(rows, -1)


def unpack_attention(flat, kinds, heads, size):
    rows = flat.shape[0]
    both = flat.reshape(rows, 2, kinds + 1, heads // 2, size)
    both = jnp.transpose(both, (2, 1, 3, 0, 4)).reshape(kinds + 1, heads, rows, size)
    return both[:kinds], jnp.transpose(both[kinds], (0, 2, 1))


def per_device(
    inputs,
    cotangent,
    segments,
    w_qkv,
    w_out,
    w_up,
    w_down,
    b_qv,
    b_up,
    ln_gain,
    ln_bias,
    res_bias,
    m_qkv,
    m_out,
    m_up,
    m_down,
    m_bqv,
    m_bup,
    m_gain,
    m_lnbias,
    m_res,
):
    dp = lax.axis_size("dp")
    ring = Ring(dp)
    core = ring.core
    kinds, heads, rows, size = w_qkv.shape
    own_heads = heads // 2
    tokens, width = inputs.shape
    hidden = w_up.shape[1] // 2
    scaling = float(size) ** (-0.5)
    grad_scale = float(dp * tokens) ** (-0.5)

    vectors = (b_qv, b_up, ln_gain, ln_bias, res_bias)
    sizes = [math.prod(v.shape) for v in vectors]
    cuts = [sum(sizes[:i]) for i in range(len(sizes) + 1)]
    packed = jnp.concatenate([v.reshape(-1) for v in vectors]).astype(bf16)
    everyone = lax.all_gather(packed[None], "dp", axis=0, tiled=True).astype(f32)

    def vector(i, leading):
        part = everyone[:, cuts[i] : cuts[i + 1]].reshape((dp,) + leading + (-1,))
        return jnp.moveaxis(part, 0, len(leading)).reshape(leading + (-1,))

    bqv_all = vector(0, b_qv.shape[:2])
    bqv = lax.dynamic_slice_in_dim(bqv_all, core * own_heads, own_heads, 1)
    bup = lax.dynamic_slice_in_dim(vector(1, ()), core * hidden, hidden, 0)
    gain, bias, res = vector(2, (2,)), vector(3, (2,)), vector(4, ())

    cot = jnp.concatenate([cotangent, ring.swap(cotangent)], axis=0)
    x_own = inputs.astype(f32)
    x_hat, inv_std = normalize(x_own)
    other_hat, _ = normalize(ring.swap(inputs).astype(f32))
    hats = jnp.concatenate([x_hat, other_hat], axis=0)
    act_one = (hats * gain[0] + bias[0]).astype(bf16)
    act_two = (hats * gain[1] + bias[1]).astype(bf16)
    segs = jnp.concatenate([segments, ring.swap(segments)], axis=0)
    allowed, cos_b, sin_b = rotary_tables(segs, ROT)

    att_rows = pack_attention(w_qkv.astype(bf16), w_out.astype(bf16))
    down_rows = w_down.astype(bf16).T
    w_att, marks = ring.gather(att_rows, 1)
    w_u, marks = ring.gather(w_up.astype(bf16), 1, marks[-2])
    w_d, marks = ring.gather(down_rows, 1, marks[-2])
    cut = kinds * own_heads * size
    w_in, w_o = w_att[:, :cut], w_att[:, cut:]

    qkv = nn(act_one, w_in).reshape(2, tokens, kinds, own_heads, size)
    q = rotate(qkv[:, :, 0] + bqv[0], cos_b, sin_b).astype(bf16)
    k = rotate(qkv[:, :, 1], cos_b, sin_b).astype(bf16)
    v = (qkv[:, :, 2] + bqv[1]).astype(bf16)
    o, prob = attention(q, k, v, allowed, scaling)
    do = nn(cot, w_o).astype(bf16).reshape(o.shape)
    dq, dk, dv = attention_back(q, k, v, o, do, prob, scaling)
    dq = rotate(dq, cos_b, -sin_b)
    dk = rotate(dk, cos_b, -sin_b)
    own_bqv = jnp.stack([jnp.sum(dq, axis=(0, 1)), jnp.sum(dv, axis=(0, 1))])
    dqkv = jnp.stack([dq, dk, dv], axis=2).astype(bf16).reshape(2 * tokens, cut)
    o = o.reshape(2 * tokens, own_heads * size)
    g_att = jnp.concatenate(
        [(tn(act_one, dqkv) * grad_scale).astype(bf16), (tn(cot, o) * grad_scale).astype(bf16)], axis=1
    )

    pre_act = nn(act_two, w_u) + bup
    hid, slope = gelu_parts(pre_act)
    hid = hid.astype(bf16)
    g_down = (tn(cot, hid) * grad_scale).astype(bf16)
    du = nn(cot, w_d) * slope
    own_bup = jnp.sum(du, axis=0)
    du_b = du.astype(bf16)
    g_up = (tn(act_two, du_b) * grad_scale).astype(bf16)

    sum_att = ring.reduce(g_att, rows, 1)
    sum_down = ring.reduce(g_down, rows, 1)
    sum_up = ring.reduce(g_up, rows, 1)
    mom_att = momentum_beta * pack_attention(m_qkv, m_out) + sum_att
    mom_down = momentum_beta * m_down.T + sum_down
    mom_up = momentum_beta * m_up + sum_up
    step_size = matrix_rate * 0.2 * math.sqrt(MODEL_WIDTH)
    upd_qkv, upd_out = unpack_attention(muon_update(mom_att, size), kinds, heads, size)
    upd_down = muon_update(mom_down, size).T
    upd_up = muon_update(mom_up, size)
    new_qkv = w_qkv - step_size * upd_qkv.astype(f32)
    new_out = w_out - step_size * upd_out.astype(f32)
    new_down = w_down - step_size * upd_down.astype(f32)
    new_up = w_up - step_size * upd_up.astype(f32)
    grad_qkv, grad_out = unpack_attention(sum_att, kinds, heads, size)
    mom_qkv, mom_out = unpack_attention(mom_att, kinds, heads, size)

    branch = combine(ring, nt(o, w_o) + nt(hid, w_d))
    output = (x_own + branch + res).astype(bf16)
    da_one = combine(ring, nt(dqkv, w_in))
    da_two = combine(ring, nt(du_b, w_u))
    cot_own = cotangent.astype(f32)
    dx_one, gain_one, bias_one = norm_reverse_pass(da_one, x_hat, inv_std, gain[0])
    dx_two, gain_two, bias_two = norm_reverse_pass(da_two, x_hat, inv_std, gain[1])
    input_grad = cot_own + dx_one + dx_two

    s_bqv = lax.dynamic_update_slice_in_dim(jnp.zeros_like(bqv_all), own_bqv, core * own_heads, 1)
    s_bup = lax.dynamic_update_slice_in_dim(jnp.zeros((2 * hidden,), f32), own_bup, core * hidden, 0)
    sums = (s_bqv, s_bup, jnp.stack([gain_one, gain_two]), jnp.stack([bias_one, bias_two]), jnp.sum(cot_own, axis=0))
    pieces = [
        jnp.moveaxis(s.reshape(s.shape[:-1] + (dp, -1)), -2, 0).reshape(dp, -1) for s in sums
    ]
    spread = lax.all_to_all(
        jnp.concatenate(pieces, axis=1) * grad_scale, "dp", split_axis=0, concat_axis=0, tiled=True
    )
    total = jnp.sum(spread, axis=0)
    vec_grads = [total[cuts[i] : cuts[i + 1]].reshape(v.shape) for i, v in enumerate(vectors)]
    vec_moms = [momentum_beta * m + g for m, g in zip((m_bqv, m_bup, m_gain, m_lnbias, m_res), vec_grads)]
    vec_news = [v - vector_rate * m for v, m in zip(vectors, vec_moms)]

    return (
        output,
        input_grad,
        grad_qkv,
        grad_out,
        sum_up,
        sum_down.T,
        *vec_grads,
        new_qkv,
        new_out,
        new_up,
        new_down,
        *vec_news,
        mom_qkv,
        mom_out,
        mom_up,
        mom_down.T,
        *vec_moms,
    )


def solution(mesh):
    tokens = (P("dp", None), P("dp", None))
    matrices = (
        P(None, "tensor", "dp", None),
        P("tensor", None, "dp"),
        P("dp", "tensor"),
        P("tensor", "dp"),
    )
    vectors = (
        P(None, "tensor", "dp"),
        P(("tensor", "dp")),
        P(None, "dp"),
        P(None, "dp"),
        P("dp"),
    )
    return jax.shard_map(
        per_device,
        mesh=mesh,
        in_specs=tokens + (P("dp", None),) + (matrices + vectors) * 2,
        out_specs=tokens + (matrices + vectors) * 3,
        check_vma=False,
    )
```

```python
import math

import jax
import jax.numpy as jnp
from jax import lax
from jax.experimental import pallas as pl
from jax.sharding import PartitionSpec as P


MODEL_WIDTH = 2048
ROT = 64
NS_ITERS = 5

norm_eps = 1e-05
momentum_beta = 0.9
matrix_rate = 0.1
vector_rate = 0.4
coef_one = 3.4445
coef_two = -4.775
coef_three = 2.0315
big_negative = -1e30

bf16 = jnp.bfloat16
f32 = jnp.float32

INTERPRET = False


def dot(a, b, dims):
    return lax.dot_general(a, b, (dims, ((), ())), preferred_element_type=f32)


def nn(a, b):
    return dot(a, b, ((1,), (0,)))


def nt(a, b):
    return dot(a, b, ((1,), (1,)))


def tn(a, b):
    return dot(a, b, ((0,), (0,)))


QUAD = (4, 1)


def exchange(value):
    return lax.all_to_all(value, "dp", split_axis=0, concat_axis=0, tiled=True)


class Group:
    def __init__(self, dp):
        self.dp = dp
        self.index = lax.axis_index("dp")
        bits = [1 << i for i in range(dp.bit_length())][: dp.bit_length() - 1]
        self.bits = bits[::-1]
        self.sums = [b for b in bits if b not in QUAD and b > QUAD[0]] + [
            b for b in bits if b not in QUAD and b < QUAD[0]
        ]

    def flip(self, value, bit):
        return lax.ppermute(value, "dp", [(i, i ^ bit) for i in range(self.dp)])

    def side(self, bit):
        return (self.index // bit) % 2

    def split(self, value, bit, axis):
        side = self.side(bit)
        return (
            lax.dynamic_index_in_dim(value, side, axis, keepdims=False),
            lax.dynamic_index_in_dim(value, 1 - side, axis, keepdims=False),
        )

    def join(self, mine, theirs, bit, axis):
        first = self.side(bit) == 0
        low = jnp.where(first, mine, theirs)
        high = jnp.where(first, theirs, mine)
        return jnp.stack([low, high], axis=axis)

    def gather(self, shard):
        _, rows, cols = shard.shape
        value = shard.reshape(2, 2, rows, cols)
        mine, theirs = self.split(value, QUAD[0], 0)
        value = self.join(mine, self.flip(theirs, QUAD[0]), QUAD[0], 0)
        mine, theirs = self.split(value, QUAD[1], 1)
        value = self.join(mine, self.flip(theirs, QUAD[1]), QUAD[1], 1)
        held = list(QUAD)
        for bit in self.sums:
            axis = sum(b > bit for b in held)
            value = self.join(value, self.flip(value, bit), bit, axis)
            held = sorted(held + [bit], reverse=True)
        return value.reshape(self.dp * rows, cols)

    def reduce(self, grad):
        cols = grad.shape[1]
        rows = grad.shape[0] // self.dp
        held = list(self.bits)
        value = grad.reshape([2] * len(held) + [rows, cols])
        for bit in self.sums[::-1]:
            axis = held.index(bit)
            mine, theirs = self.split(value, bit, axis)
            value = (mine.astype(f32) + self.flip(theirs, bit).astype(f32)).astype(bf16)
            held.remove(bit)
        mine, theirs = self.split(value, QUAD[0], 0)
        value = self.join(mine, self.flip(theirs, QUAD[0]), QUAD[0], 0)
        mine, theirs = self.split(value, QUAD[1], 1)
        value = self.join(mine, self.flip(theirs, QUAD[1]), QUAD[1], 1)
        return value.reshape(4, rows, cols)

    def across(self, value):
        return lax.ppermute(value, "tensor", [(0, 1), (1, 0)])

    def tokens(self, value):
        half = value.shape[0] // 2
        if lax.axis_size("tensor") == 2 and half:
            side = lax.axis_index("tensor")
            mine = lax.dynamic_slice_in_dim(value, side * half, half, 0)
            mine = self.flip(mine, QUAD[0])
            other = self.across(mine)
            low, high = jnp.where(side == 0, mine, other), jnp.where(side == 0, other, mine)
            value = jnp.concatenate([value, low, high], axis=0)
        else:
            value = jnp.concatenate([value, self.flip(value, QUAD[0])], axis=0)
        return jnp.concatenate([value, self.flip(value, QUAD[1])], axis=0)

    def own_tokens(self, partial):
        half = partial.shape[0] // 2
        width = partial.shape[1] // 2
        theirs = self.flip(partial[half:].astype(bf16), QUAD[1])
        partial = partial[:half] + theirs.astype(f32)
        if lax.axis_size("tensor") == 2:
            side = lax.axis_index("tensor")
            partial = partial.astype(bf16)
            mine = lax.dynamic_slice_in_dim(partial, side * width, width, 1)
            theirs = lax.dynamic_slice_in_dim(partial, (1 - side) * width, width, 1)
            partial = mine.astype(f32) + self.across(theirs).astype(f32)
        half = half // 2
        theirs = self.flip(partial[half:].astype(bf16), QUAD[0])
        partial = (partial[:half] + theirs.astype(f32)).astype(bf16)
        if lax.axis_size("tensor") == 2:
            other = self.across(partial)
            low, high = jnp.where(side == 0, partial, other), jnp.where(side == 0, other, partial)
            return jnp.concatenate([low, high], axis=1).astype(f32)
        return lax.psum(partial, "tensor").astype(f32)


def normalize(values):
    centred = values - jnp.mean(values, axis=-1, keepdims=True)
    inv_std = lax.rsqrt(jnp.mean(centred * centred, axis=-1, keepdims=True) + norm_eps)
    return centred * inv_std, inv_std


def norm_reverse_pass(grad_in, x_hat, inv_std, gain_row):
    scaled_g = grad_in * gain_row
    mean_g = jnp.mean(scaled_g, axis=-1, keepdims=True)
    mean_gx = jnp.mean(scaled_g * x_hat, axis=-1, keepdims=True)
    return (
        inv_std * (scaled_g - mean_g - x_hat * mean_gx),
        jnp.sum(grad_in * x_hat, axis=0),
        jnp.sum(grad_in, axis=0),
    )


def rotary_tables(seg_ids, rot_dims):
    order_idx = jnp.arange(seg_ids.shape[1], dtype=jnp.int32)
    causal = order_idx[:, None] >= order_idx[None, :]
    allowed = (seg_ids[:, :, None] == seg_ids[:, None, :]) & causal[None]
    position = (jnp.sum(allowed.astype(jnp.int32), axis=2) - 1).astype(f32)
    freq_idx = jnp.arange(rot_dims // 2, dtype=f32)
    inv_freq = jnp.exp(freq_idx * (-2.0 * math.log(10000.0) / rot_dims))
    angles = position[:, :, None] * inv_freq
    return allowed, jnp.cos(angles)[:, :, None, :], jnp.sin(angles)[:, :, None, :]


def rotate(values, cos_b, sin_b):
    half_dim = cos_b.shape[-1]
    low = values[..., :half_dim]
    high = values[..., half_dim : 2 * half_dim]
    return jnp.concatenate(
        [low * cos_b - high * sin_b, high * cos_b + low * sin_b, values[..., 2 * half_dim :]], axis=-1
    )


def gelu_parts(pre_act):
    cdf = 0.5 * (1.0 + lax.erf(pre_act * (1.0 / math.sqrt(2.0))))
    pdf = jnp.exp(-0.5 * pre_act * pre_act) * (1.0 / math.sqrt(2.0 * math.pi))
    return pre_act * cdf, cdf + pre_act * pdf


def attention(q, k, v, allowed, scaling):
    scores = jnp.einsum("slhe,smhe->shlm", q, k, preferred_element_type=f32) * scaling
    masked = jnp.where(allowed[:, None], scores, big_negative)
    top = jnp.max(masked, axis=-1, keepdims=True)
    log_sum = top + jnp.log(jnp.sum(jnp.exp(masked - top), axis=-1, keepdims=True))
    prob = jnp.exp(masked - log_sum)
    out = jnp.einsum("shlm,smhe->slhe", prob.astype(bf16), v, preferred_element_type=f32)
    return out.astype(bf16), prob


def attention_back(q, k, v, o, do, prob, scaling):
    dprob = jnp.einsum("slhe,smhe->shlm", do, v, preferred_element_type=f32)
    delta = jnp.sum(do.astype(f32) * o.astype(f32), axis=-1)
    dscore = (prob * (dprob - jnp.transpose(delta, (0, 2, 1))[..., None]) * scaling).astype(bf16)
    dq = jnp.einsum("shlm,smhe->slhe", dscore, k, preferred_element_type=f32)
    dk = jnp.einsum("shlm,slhe->smhe", dscore, q, preferred_element_type=f32)
    dv = jnp.einsum("shlm,slhe->smhe", prob.astype(bf16), do, preferred_element_type=f32)
    return dq, dk, dv


def series_kernel(gram_ref, out_ref):
    def mul(a, b):
        return jnp.dot(a, b, preferred_element_type=f32, precision=lax.Precision.HIGHEST)

    gram = gram_ref[0]
    size = gram.shape[0]
    row = lax.broadcasted_iota(jnp.int32, (size, size), 0)
    col = lax.broadcasted_iota(jnp.int32, (size, size), 1)
    diagonal = row == col
    trace = jnp.sum(jnp.where(diagonal, gram, 0.0), axis=(0, 1), keepdims=True)
    inverse = 1.0 / (jnp.sqrt(trace) + 1e-07)
    gram = gram * inverse * inverse
    total = jnp.where(diagonal, 1.0, 0.0) * inverse
    for turn in range(NS_ITERS):
        poly = coef_two * gram + coef_three * mul(gram, gram)
        if turn == 0:
            total = coef_one * total + poly * inverse
        else:
            total = coef_one * total + mul(total, poly)
        if turn < NS_ITERS - 1:
            once = coef_one * gram + mul(gram, poly)
            gram = coef_one * once + mul(once, poly)
    out_ref[0] = total.astype(out_ref.dtype)


def series(grams):
    count, size, _ = grams.shape
    spec = pl.BlockSpec((1, size, size), lambda i: (i, 0, 0))
    return pl.pallas_call(
        series_kernel,
        grid=(count,),
        in_specs=[spec],
        out_specs=spec,
        out_shape=jax.ShapeDtypeStruct(grams.shape, bf16),
        interpret=INTERPRET,
        name="series",
    )(grams)


def muon_update(blocks):
    count, rows, size = blocks.shape
    dp = lax.axis_size("dp")
    slots = -(-count // dp)
    if slots * dp != count:
        blocks = jnp.pad(blocks, ((0, slots * dp - count), (0, 0), (0, 0)))
    blocks = blocks.reshape(dp, slots, rows, size)
    whole = exchange(blocks)
    whole = jnp.swapaxes(whole, 0, 1).reshape(slots, dp * rows, size)
    grams = jnp.einsum("ndf,ndg->nfg", whole, whole, preferred_element_type=f32)
    done = jnp.einsum("ndf,nfg->ndg", whole, series(grams), preferred_element_type=f32).astype(bf16)
    done = jnp.swapaxes(done.reshape(slots, dp, rows, size), 0, 1)
    back = exchange(done)
    return back.reshape(slots * dp, rows, size)[:count]


def pack_attention(qkv, out):
    kinds, heads, rows, size = qkv.shape
    both = jnp.concatenate([qkv, jnp.transpose(out, (0, 2, 1))[None]], axis=0)
    both = both.reshape(kinds + 1, 4, heads // 4, rows, size)
    return jnp.transpose(both, (1, 3, 0, 2, 4)).reshape(4, rows, -1)


def pack_columns(flat):
    return jnp.swapaxes(flat.reshape(flat.shape[0], 4, -1), 0, 1)


def to_blocks(quarters, size):
    _, rows, cols = quarters.shape
    parts = quarters.reshape(4, rows, cols // size, size)
    return jnp.swapaxes(parts, 1, 2).reshape(-1, rows, size)


def attention_from_blocks(blocks, kinds, heads):
    rows, size = blocks.shape[1:]
    both = blocks.reshape(4, kinds + 1, heads // 4, rows, size)
    both = jnp.swapaxes(both, 0, 1).reshape(kinds + 1, heads, rows, size)
    return both[:kinds], jnp.swapaxes(both[kinds], 1, 2)


def columns_from_blocks(blocks):
    return jnp.swapaxes(blocks, 0, 1).reshape(blocks.shape[1], -1)


def rows_from_blocks(blocks):
    return jnp.swapaxes(blocks, 1, 2).reshape(-1, blocks.shape[1])


def per_device(
    inputs,
    cotangent,
    segments,
    w_qkv,
    w_out,
    w_up,
    w_down,
    b_qv,
    b_up,
    ln_gain,
    ln_bias,
    res_bias,
    m_qkv,
    m_out,
    m_up,
    m_down,
    m_bqv,
    m_bup,
    m_gain,
    m_lnbias,
    m_res,
):
    dp = lax.axis_size("dp")
    group = Group(dp)
    quarter = 2 * group.side(QUAD[0]) + group.side(QUAD[1])
    kinds, heads, _, size = w_qkv.shape
    own_heads = heads // 4
    tokens, _ = inputs.shape
    hidden = w_up.shape[1] // 4
    scaling = float(size) ** (-0.5)
    grad_scale = float(dp * tokens) ** (-0.5)

    c_qkv, c_out, c_up, c_down = (
        w.astype(bf16) for w in lax.optimization_barrier((w_qkv, w_out, w_up, w_down))
    )
    w_att = group.gather(pack_attention(c_qkv, c_out))
    w_u = group.gather(pack_columns(c_up))
    w_d = group.gather(pack_columns(c_down.T))
    cut = kinds * own_heads * size

    m_qkv, m_out, m_up, m_down, w_att = lax.optimization_barrier((m_qkv, m_out, m_up, m_down, w_att))

    w_in, w_o = w_att[:, :cut], w_att[:, cut:]

    vectors = (b_qv, b_up, ln_gain, ln_bias, res_bias)
    sizes = [math.prod(v.shape) for v in vectors]
    cuts = [sum(sizes[:i]) for i in range(len(sizes) + 1)]
    packed = jnp.concatenate([v.reshape(-1) for v in vectors]).astype(bf16)
    everyone = exchange(jnp.broadcast_to(packed, (dp,) + packed.shape))
    everyone = lax.optimization_barrier((everyone, w_att))[0].astype(f32)

    def vector(i, leading):
        part = everyone[:, cuts[i] : cuts[i + 1]].reshape((dp,) + leading + (-1,))
        return jnp.moveaxis(part, 0, len(leading)).reshape(leading + (-1,))

    bqv_all = vector(0, b_qv.shape[:2])
    bqv = lax.dynamic_slice_in_dim(bqv_all, quarter * own_heads, own_heads, 1)
    bup = lax.dynamic_slice_in_dim(vector(1, ()), quarter * hidden, hidden, 0)
    gain, bias, res = vector(2, (2,)), vector(3, (2,)), vector(4, ())

    cot = group.tokens(cotangent)
    x_all = group.tokens(inputs)
    hats, inv_all = normalize(x_all.astype(f32))
    x_hat, inv_std = hats[:tokens], inv_all[:tokens]
    act_one = (hats * gain[0] + bias[0]).astype(bf16)
    act_two = (hats * gain[1] + bias[1]).astype(bf16)
    allowed, cos_b, sin_b = rotary_tables(group.tokens(segments), ROT)

    qkv = nn(act_one, w_in).reshape(4, tokens, kinds, own_heads, size)
    q = rotate(qkv[:, :, 0] + bqv[0], cos_b, sin_b).astype(bf16)
    k = rotate(qkv[:, :, 1], cos_b, sin_b).astype(bf16)
    v = (qkv[:, :, 2] + bqv[1]).astype(bf16)
    o, prob = attention(q, k, v, allowed, scaling)
    do = nn(cot, w_o).astype(bf16).reshape(o.shape)
    dq, dk, dv = attention_back(q, k, v, o, do, prob, scaling)
    dq = rotate(dq, cos_b, -sin_b)
    dk = rotate(dk, cos_b, -sin_b)
    own_bqv = jnp.stack([jnp.sum(dq, axis=(0, 1)), jnp.sum(dv, axis=(0, 1))])
    dqkv = jnp.stack([dq, dk, dv], axis=2).astype(bf16).reshape(4 * tokens, cut)
    o = o.reshape(4 * tokens, own_heads * size)
    g_att = jnp.concatenate(
        [(tn(act_one, dqkv) * grad_scale).astype(bf16), (tn(cot, o) * grad_scale).astype(bf16)], axis=1
    )

    pre_act = nn(act_two, w_u) + bup
    hid, slope = gelu_parts(pre_act)
    hid = hid.astype(bf16)
    g_down = (tn(cot, hid) * grad_scale).astype(bf16)
    du = nn(cot, w_d) * slope
    own_bup = jnp.sum(du, axis=0)
    du_b = du.astype(bf16)
    g_up = (tn(act_two, du_b) * grad_scale).astype(bf16)

    step_size = matrix_rate * 0.2 * math.sqrt(MODEL_WIDTH)
    s_att = to_blocks(group.reduce(g_att), size)
    s_down = to_blocks(group.reduce(g_down), size)
    s_up = to_blocks(group.reduce(g_up), size)

    def blocks_momentum(packed_momentum, s):
        return (momentum_beta * to_blocks(packed_momentum, size) + s.astype(f32)).astype(bf16)

    u_att = muon_update(blocks_momentum(pack_attention(m_qkv, m_out), s_att))
    u_down = muon_update(blocks_momentum(pack_columns(m_down.T), s_down))
    u_up = muon_update(blocks_momentum(pack_columns(m_up), s_up))
    grad_qkv, grad_out = attention_from_blocks(s_att, kinds, heads)
    mat_grads = [
        g.astype(f32) for g in (grad_qkv, grad_out, columns_from_blocks(s_up), rows_from_blocks(s_down))
    ]
    mat_moms = [momentum_beta * m + g for m, g in zip((m_qkv, m_out, m_up, m_down), mat_grads)]
    upd_qkv, upd_out = attention_from_blocks(u_att, kinds, heads)
    updates = (upd_qkv, upd_out, columns_from_blocks(u_up), rows_from_blocks(u_down))
    mat_news = [w - step_size * u.astype(f32) for w, u in zip((w_qkv, w_out, w_up, w_down), updates)]

    x_own = inputs.astype(f32)
    branch = group.own_tokens(nt(o, w_o) + nt(hid, w_d))
    output = (x_own + branch + res).astype(bf16)
    da_one = group.own_tokens(nt(dqkv, w_in))
    da_two = group.own_tokens(nt(du_b, w_u))
    cot_own = cotangent.astype(f32)
    dx_one, gain_one, bias_one = norm_reverse_pass(da_one, x_hat, inv_std, gain[0])
    dx_two, gain_two, bias_two = norm_reverse_pass(da_two, x_hat, inv_std, gain[1])
    input_grad = cot_own + dx_one + dx_two

    s_bqv = lax.dynamic_update_slice_in_dim(jnp.zeros_like(bqv_all), own_bqv, quarter * own_heads, 1)
    s_bup = lax.dynamic_update_slice_in_dim(jnp.zeros((4 * hidden,), f32), own_bup, quarter * hidden, 0)
    sums = (s_bqv, s_bup, jnp.stack([gain_one, gain_two]), jnp.stack([bias_one, bias_two]), jnp.sum(cot_own, axis=0))
    pieces = [
        jnp.moveaxis(s.reshape(s.shape[:-1] + (dp, -1)), -2, 0).reshape(dp, -1) for s in sums
    ]
    spread = exchange(jnp.concatenate(pieces, axis=1) * grad_scale)
    total = jnp.sum(spread, axis=0)
    vec_grads = [total[cuts[i] : cuts[i + 1]].reshape(v.shape) for i, v in enumerate(vectors)]
    vec_moms = [momentum_beta * m + g for m, g in zip((m_bqv, m_bup, m_gain, m_lnbias, m_res), vec_grads)]
    vec_news = [v - vector_rate * m for v, m in zip(vectors, vec_moms)]

    return (output, input_grad, *mat_grads, *vec_grads, *mat_news, *vec_news, *mat_moms, *vec_moms)


def solution(mesh):
    tokens = (P("dp", None), P("dp", None))
    matrices = (
        P(None, "tensor", "dp", None),
        P("tensor", None, "dp"),
        P("dp", "tensor"),
        P("tensor", "dp"),
    )
    vectors = (
        P(None, "tensor", "dp"),
        P(("tensor", "dp")),
        P(None, "dp"),
        P(None, "dp"),
        P("dp"),
    )
    return jax.shard_map(
        per_device,
        mesh=mesh,
        in_specs=tokens + (P("dp", None),) + (matrices + vectors) * 2,
        out_specs=tokens + (matrices + vectors) * 3,
        check_vma=False,
    )
```
